32 devices in a mesh: gx: 8 (over y, x, core), gy: 4 (over z).
Axes of the slice: x: 2, y: 2, z: 4, core: 2. Of those that a mesh axis runs over, the one named last changes fastest.
Arguments:
- x_first: bfloat16 [128, 16384], P(None, 'gx'), may hold values from -160 to 160
- x_second: bfloat16 [128, 16384], P(None, 'gx'), may hold values from -160 to 160
- norm_gain: bfloat16 [16384], P('gx'), may hold values from 0.25 to 1.75
- w_qkv: bfloat16 [16384, 18432], P('gx', 'gy'), may hold values from -0.046875 to 0.046875
- w_out: bfloat16 [16384, 16384], P('gy', 'gx'), may hold values from -0.046875 to 0.046875
- cache_keys: bfloat16 [128, 768, 1024], P(('gx', 'gy')), may hold values from -240 to 240
- cache_values: bfloat16 [128, 768, 1024], P(('gx', 'gy')), may hold values from -8 to 8
- lengths: int32 [128], P(('gx', 'gy')), may hold values from 1 to 768, as said below
Outputs:
- out_first: bfloat16 [128, 16384], P('gy', 'gx')
- out_second: bfloat16 [128, 16384], P('gy', 'gx')
The draws below stay inside these ranges and needn't reach their ends.
Inputs may be any that keep to these rules, and one draw needn't show every extreme that they name: `lengths`: some sequence has exactly 768 filled slots in every draw.
All inputs are finite; a program needn't handle non-finite values.
Results may differ from the reference program's by a relative error of at most 0.012.
The reference program's roundings to bfloat16 on the way count: a program that leaves them out, or rounds other values in their place, can miss the bound.
Values may be sent and summed in bfloat16 or wider, within the bound.
A program may use at most 192 MiB of HBM per device.

```python
import math
import jax
import jax.numpy as jnp
from jax import lax

D = 16384
HEADS = 128
KVH = 8
HD = 128
CACHE = 768
BATCH = 128
GROUP = 16


def draw_inputs(key, salt):
    key = jax.random.fold_in(key, salt)
    noise_key, column_key, row_key = jax.random.split(key, 3)
    noise = jnp.clip(jax.random.normal(noise_key, (BATCH, D), jnp.float32), -4.0, 4.0)
    rise = 3.0
    column = jnp.arange(D, dtype=jnp.float32) / D
    column_scale = rise ** column * jnp.exp(jax.random.uniform(column_key, (D,), jnp.float32, 0.0, math.log(3.3)))
    row_scale = jnp.exp(jax.random.uniform(row_key, (BATCH, 1), jnp.float32, math.log(0.3), math.log(3.0)))
    return (noise * column_scale[None, :] * row_scale).astype(jnp.bfloat16)


def draw_x_first(key, part):
    return draw_inputs(key, 101)


def draw_x_second(key, part):
    return draw_inputs(key, 202)


def draw_cache_keys(key, part):
    key = jax.random.fold_in(key, 303)
    noise_key = jax.random.fold_in(key, 0)
    noise = jnp.clip(jax.random.normal(noise_key, (BATCH, CACHE, KVH * HD), jnp.float32), -4.0, 4.0)
    return noise.astype(jnp.bfloat16)


def draw_cache_values(key, part):
    key = jax.random.fold_in(key, 404)
    offset_key, noise_key = jax.random.split(key)
    offset = jnp.clip(jax.random.normal(offset_key, (BATCH, 1, KVH * HD), jnp.float32), -4.0, 4.0)
    noise = jnp.clip(jax.random.normal(noise_key, (BATCH, CACHE, KVH * HD), jnp.float32), -4.0, 4.0)
    return (offset + noise).astype(jnp.bfloat16)


def draw_lengths(key, part):
    key = jax.random.fold_in(key, 505)
    first_key, second_key, third_key, pick_key = jax.random.split(key, 4)
    first = jax.random.randint(first_key, (BATCH,), 1, CACHE + 1)
    second = jax.random.randint(second_key, (BATCH,), 1, CACHE + 1)
    third = jax.random.randint(third_key, (BATCH,), 1, CACHE + 1)
    shortest = jnp.minimum(jnp.minimum(first, second), third)
    chosen = jax.random.randint(pick_key, (), 0, BATCH)
    return jnp.where(jnp.arange(BATCH, dtype=jnp.int32) == chosen, CACHE, shortest).astype(jnp.int32)


def shard_levels(rng, shape, shards, least, high):
    def one(dim, parts):
        steps = jax.random.uniform(jax.random.fold_in(jax.random.fold_in(rng, 6), dim), (parts,), jnp.float32, least / len(shards), high / len(shards))
        return jnp.repeat(jnp.exp(steps), shape[dim] // parts).reshape((-1,) + (1,) * (len(shape) - dim - 1))

    loudness = one(*shards[0])
    for cut in shards[1:]:
        loudness = loudness * one(*cut)
    return loudness


def centred(rng, shape, deviation, bound, shards=(), kind=jnp.bfloat16):
    result = jax.random.normal(rng, shape, jnp.float32) * deviation
    if len(shards) > 0:
        result = shard_levels(rng, shape, shards, -0.22, 0.18) * result
    return jnp.clip(result, min=-bound, max=bound).astype(kind)


def setup_inputs(seed: int = 0) -> dict:
    key_list = jax.random.split(jax.random.key(seed), 9)
    return {
        "x_first": draw_x_first(jax.random.fold_in(key_list[8], 71), 0),
        "x_second": draw_x_second(jax.random.fold_in(key_list[8], 71), 0),
        "norm_gain": jnp.clip(1.0 + 0.15 * jax.random.normal(key_list[2], (D,), jnp.float32), 0.25, 1.75).astype(jnp.bfloat16),
        "w_qkv": centred(key_list[3], (D, (HEADS + 2 * KVH) * HD), D ** -0.5, 0.046875, ((0, 8), (1, 4))),
        "w_out": centred(key_list[4], (HEADS * HD, D), (HEADS * HD) ** -0.5, 0.046875, ((0, 4), (1, 8))),
        "cache_keys": draw_cache_keys(jax.random.fold_in(key_list[8], 71), 0),
        "cache_values": draw_cache_values(jax.random.fold_in(key_list[8], 71), 0),
        "lengths": draw_lengths(jax.random.fold_in(key_list[8], 71), 0),
    }


norm_eps = 1e-05
rotary_base = 500000.0

def rotate_pairs(values, position):
    half_width = values.shape[-1] // 2
    freq = rotary_base ** (-(jnp.arange(half_width, dtype=jnp.float32) * 2.0 / values.shape[-1]))
    angle = position.astype(jnp.float32)[..., None] * freq
    shape = position.shape + (1,) * (values.ndim - position.ndim - 1) + (half_width,)
    cosine = jnp.cos(angle).reshape(shape)
    sine = jnp.sin(angle).reshape(shape)
    first = values[..., :half_width]
    second = values[..., half_width:]
    return jnp.concatenate([first * cosine - second * sine, second * cosine + first * sine], axis=-1)

def project(x_rows, norm_gain, w_qkv):
    wide = x_rows.astype(jnp.float32)
    squares = lax.optimization_barrier(jnp.sum(wide * wide, axis=1))
    row_scale = lax.rsqrt(squares / D + norm_eps)
    scaled = (wide * norm_gain.astype(jnp.float32)[None, :]).astype(jnp.bfloat16)
    partial_sum = jnp.dot(scaled, w_qkv, preferred_element_type=jnp.float32)
    joined = (partial_sum * row_scale[:, None]).astype(jnp.bfloat16)
    joined = joined.reshape(BATCH, KVH, GROUP + 2, HD)
    return (joined[:, :, :GROUP], joined[:, :, GROUP], joined[:, :, GROUP + 1])

def attend_row(packed):
    query, keys_cache, values_cache, length, extra_keys, extra_values = packed
    score_scale = 1.0 / math.sqrt(HD)
    query_wide = query.astype(jnp.float32)
    keys_wide = keys_cache.astype(jnp.float32).reshape(CACHE, KVH, HD)
    values_wide = values_cache.astype(jnp.float32).reshape(CACHE, KVH, HD)
    cache_scores = jnp.einsum('kgd,tkd->kgt', query_wide, keys_wide) * score_scale
    valid = jnp.arange(CACHE, dtype=jnp.int32) < length
    cache_scores = jnp.where(valid[None, None, :], cache_scores, -jnp.inf)
    extra_scores = jnp.einsum('kgd,ekd->kge', query_wide, extra_keys.astype(jnp.float32)) * score_scale
    top = jnp.maximum(lax.optimization_barrier(jnp.max(cache_scores, axis=-1)), lax.optimization_barrier(jnp.max(extra_scores, axis=-1)))[..., None]
    cache_weights = jnp.exp(cache_scores - top)
    extra_weights = jnp.exp(extra_scores - top)
    total = lax.optimization_barrier(jnp.sum(cache_weights, axis=-1)) + lax.optimization_barrier(jnp.sum(extra_weights, axis=-1))
    cache_round = lax.optimization_barrier(cache_weights.astype(jnp.bfloat16)).astype(jnp.float32)
    extra_round = lax.optimization_barrier(extra_weights.astype(jnp.bfloat16)).astype(jnp.float32)
    mixed = jnp.einsum('kgt,tkd->kgd', cache_round, values_wide)
    mixed = mixed + jnp.einsum('kge,ekd->kgd', extra_round, extra_values.astype(jnp.float32))
    return (mixed / total[..., None]).astype(jnp.bfloat16).reshape(HEADS * HD)

def reference(x_first, x_second, norm_gain, w_qkv, w_out, cache_keys, cache_values, lengths):
    query_one, key_one, value_one = project(x_first, norm_gain, w_qkv)
    query_two, key_two, value_two = project(x_second, norm_gain, w_qkv)
    position_one = lengths
    position_two = lengths + 1
    query_one = rotate_pairs(query_one.astype(jnp.float32), position_one).astype(jnp.bfloat16)
    key_one = rotate_pairs(key_one.astype(jnp.float32), position_one).astype(jnp.bfloat16)
    query_two = rotate_pairs(query_two.astype(jnp.float32), position_two).astype(jnp.bfloat16)
    key_two = rotate_pairs(key_two.astype(jnp.float32), position_two).astype(jnp.bfloat16)
    heads_one = lax.map(attend_row, (query_one, cache_keys, cache_values, lengths, key_one[:, None], value_one[:, None]))
    keys_both = jnp.stack([key_one, key_two], axis=1)
    values_both = jnp.stack([value_one, value_two], axis=1)
    heads_two = lax.map(attend_row, (query_two, cache_keys, cache_values, lengths, keys_both, values_both))
    out_first = jnp.dot(heads_one, w_out, preferred_element_type=jnp.float32).astype(jnp.bfloat16)
    out_second = jnp.dot(heads_two, w_out, preferred_element_type=jnp.float32).astype(jnp.bfloat16)
    return (out_first, out_second)
```

```python
import functools
import math

import jax
import jax.numpy as jnp
from jax import lax
from jax.experimental import pallas as pl
from jax.experimental.pallas import tpu as pltpu
from jax.sharding import PartitionSpec as P

HD = 128
norm_eps = 1e-05
rotary_base = 500000.0
STEPS = 2
VMEM_LIMIT = 60 * 1024 * 1024


def qkv_kernel(heads_per, x_ref, gain_ref, w_ref, out_ref, scaled_ref):
    step = pl.program_id(0)
    last = pl.num_programs(0) - 1
    outer, inner, _, tile, _ = out_ref.shape

    @pl.when(step == 0)
    def _():
        scaled_ref[...] = (
            x_ref[...].astype(jnp.float32) * gain_ref[...].astype(jnp.float32)
        ).astype(jnp.bfloat16)

    @pl.when(step < last)
    def _():
        product = jnp.dot(scaled_ref[...], w_ref[...], preferred_element_type=jnp.float32)
        for h in range(heads_per):
            out_ref[:, :, h] = product[:, h * HD : (h + 1) * HD].reshape(outer, inner, tile, HD)

    @pl.when(step == last)
    def _():
        wide = x_ref[...].astype(jnp.float32)
        squares = jnp.sum(wide * wide, axis=1, keepdims=True)
        lanes = jnp.broadcast_to(squares, (squares.shape[0], HD)).reshape(outer, inner, tile, HD)
        for h in range(heads_per):
            out_ref[:, :, h] = lanes


def qkv_partial(x, gain, w, outer, inner):
    rows, depth = x.shape
    columns = w.shape[1]
    heads_per = 2
    width = heads_per * HD
    blocks = columns // width
    tile = rows // (outer * inner)
    return pl.pallas_call(
        functools.partial(qkv_kernel, heads_per),
        grid=(blocks + 1,),
        in_specs=[
            pl.BlockSpec((rows, depth), lambda n: (0, 0)),
            pl.BlockSpec((1, depth), lambda n: (0, 0)),
            pl.BlockSpec((depth, width), lambda n: (0, jnp.minimum(n, blocks - 1))),
        ],
        out_specs=pl.BlockSpec(
            (outer, inner, heads_per, tile, HD), lambda n: (0, 0, n, 0, 0)
        ),
        out_shape=jax.ShapeDtypeStruct(
            (outer, inner, columns // HD + heads_per, tile, HD), jnp.float32
        ),
        scratch_shapes=[pltpu.VMEM((rows, depth), jnp.bfloat16)],
        compiler_params=pltpu.CompilerParams(vmem_limit_bytes=VMEM_LIMIT),
    )(x, gain, w)


def attend_kernel(
    groups, size, rows, lengths_ref, x_ref, cos_ref, sin_ref, keys_ref, values_ref, out_ref,
    in_ref, mix_ref,
):
    row = pl.program_id(0)
    tile = STEPS * rows
    per = size + 2
    slots = keys_ref.shape[1]
    scale = 1.0 / math.sqrt(HD)

    @pl.when(row == 0)
    def _():
        for k in range(groups):
            base = k * per
            turn = x_ref[base : base + size + 1].astype(jnp.float32)
            turned = turn * cos_ref[...][None] + pltpu.roll(turn, HD // 2, 2) * sin_ref[...][None]
            turned = turned.astype(jnp.bfloat16).astype(jnp.float32)
            in_ref[base * tile : (base + size + 1) * tile] = turned.reshape((size + 1) * tile, HD)
            in_ref[(base + size + 1) * tile : (base + per) * tile] = x_ref[base + size + 1].astype(
                jnp.float32
            )

    length = lengths_ref[row]
    valid = lax.broadcasted_iota(jnp.int32, (1, slots), 1) < length
    late = lax.broadcasted_iota(jnp.int32, (STEPS * size, 1), 0) >= size
    for k in range(groups):
        base = k * per * tile
        query = jnp.concatenate(
            [
                in_ref[pl.ds(base + s * rows + row, size, stride=tile), :]
                for s in range(STEPS)
            ],
            axis=0,
        )
        new_keys = [in_ref[pl.ds(base + size * tile + s * rows + row, 1), :] for s in range(STEPS)]
        new_values = [
            in_ref[pl.ds(base + (size + 1) * tile + s * rows + row, 1), :] for s in range(STEPS)
        ]
        columns = slice(k * HD, (k + 1) * HD)
        scores = (
            lax.dot_general(
                query.astype(jnp.bfloat16),
                keys_ref[0, :, columns],
                (((1,), (1,)), ((), ())),
                preferred_element_type=jnp.float32,
            )
            * scale
        )
        scores = jnp.where(valid, scores, -jnp.inf)
        extra_one = jnp.sum(query * new_keys[0], axis=1, keepdims=True) * scale
        extra_two = jnp.sum(query * new_keys[1], axis=1, keepdims=True) * scale
        extra_two = jnp.where(late, extra_two, -jnp.inf)
        top = jnp.maximum(
            jnp.max(scores, axis=1, keepdims=True), jnp.maximum(extra_one, extra_two)
        )
        weights = jnp.exp(scores - top)
        weight_one = jnp.exp(extra_one - top)
        weight_two = jnp.exp(extra_two - top)
        total = jnp.sum(weights, axis=1, keepdims=True) + weight_one + weight_two
        mixed = jnp.dot(
            weights.astype(jnp.bfloat16),
            values_ref[0, :, columns],
            preferred_element_type=jnp.float32,
        )
        mixed = (
            mixed
            + weight_one.astype(jnp.bfloat16).astype(jnp.float32) * new_values[0]
            + weight_two.astype(jnp.bfloat16).astype(jnp.float32) * new_values[1]
        )
        mixed = mixed / total
        for s in range(STEPS):
            mix_ref[pl.ds(k * size * tile + s * rows + row, size, stride=tile), :] = mixed[
                s * size : (s + 1) * size
            ]

    @pl.when(row == rows - 1)
    def _():
        out_ref[...] = mix_ref[...].reshape(out_ref.shape).astype(jnp.bfloat16)


def attend(joined, cosine, sine, keys, values, lengths):
    rows, slots, width = keys.shape
    groups = width // HD
    heads, tile, _ = joined.shape
    size = heads // groups - 2
    whole = lambda r, lens: (0, 0)
    return pl.pallas_call(
        functools.partial(attend_kernel, groups, size, rows),
        grid_spec=pltpu.PrefetchScalarGridSpec(
            num_scalar_prefetch=1,
            grid=(rows,),
            in_specs=[
                pl.BlockSpec((heads, tile, HD), lambda r, lens: (0, 0, 0)),
                pl.BlockSpec((tile, HD), whole),
                pl.BlockSpec((tile, HD), whole),
                pl.BlockSpec((1, slots, width), lambda r, lens: (r, 0, 0)),
                pl.BlockSpec((1, slots, width), lambda r, lens: (r, 0, 0)),
            ],
            out_specs=pl.BlockSpec((groups * size, tile, HD), lambda r, lens: (0, 0, 0)),
            scratch_shapes=[
                pltpu.VMEM((heads * tile, HD), jnp.float32),
                pltpu.VMEM((groups * size * tile, HD), jnp.float32),
            ],
        ),
        out_shape=jax.ShapeDtypeStruct((groups * size, tile, HD), jnp.bfloat16),
        compiler_params=pltpu.CompilerParams(vmem_limit_bytes=VMEM_LIMIT),
    )(lengths, joined, cosine, sine, keys, values)


def out_kernel(x_ref, w_ref, out_ref, flat_ref):
    @pl.when(pl.program_id(0) == 0)
    def _():
        for h in range(x_ref.shape[2]):
            flat_ref[:, h * HD : (h + 1) * HD] = (
                x_ref[:, :, h].astype(jnp.float32).reshape(flat_ref.shape[0], HD)
            ).astype(jnp.bfloat16)

    out_ref[...] = jnp.dot(flat_ref[...], w_ref[...], preferred_element_type=jnp.float32)


def out_partial(heads, w):
    outer, inner, count, tile, _ = heads.shape
    rows = outer * inner * tile
    depth, columns = w.shape
    width = min(256, columns)
    return pl.pallas_call(
        out_kernel,
        grid=(columns // width,),
        in_specs=[
            pl.BlockSpec(heads.shape, lambda n: (0, 0, 0, 0, 0)),
            pl.BlockSpec((depth, width), lambda n: (0, n)),
        ],
        out_specs=pl.BlockSpec((rows, width), lambda n: (0, n)),
        out_shape=jax.ShapeDtypeStruct((rows, columns), jnp.float32),
        scratch_shapes=[pltpu.VMEM((rows, depth), jnp.bfloat16)],
        compiler_params=pltpu.CompilerParams(vmem_limit_bytes=VMEM_LIMIT),
    )(heads, w)


def body(x_first, x_second, norm_gain, w_qkv, w_out, cache_keys, cache_values, lengths):
    outer, inner = lax.axis_size("gx"), lax.axis_size("gy")
    rows = lengths.shape[0]
    tile = STEPS * rows
    depth = x_first.shape[1]
    width = depth * outer
    heads_here = w_qkv.shape[1] // HD

    stacked = jnp.stack(
        [x.reshape(outer * inner, rows, depth) for x in (x_first, x_second)], axis=1
    ).reshape(outer * inner * tile, depth)
    half = HD // 2
    freq = rotary_base ** (-(jnp.arange(half, dtype=jnp.float32) * 2.0 / HD))
    position = jnp.concatenate([lengths + s for s in range(STEPS)])
    angle = position.astype(jnp.float32)[:, None] * freq
    cosine = jnp.tile(jnp.cos(angle), (1, 2))
    sine = jnp.concatenate([-jnp.sin(angle), jnp.sin(angle)], axis=1)

    partial_sum = qkv_partial(stacked, norm_gain[None], w_qkv, outer, inner)
    summed = lax.psum_scatter(partial_sum, "gx", scatter_dimension=0, tiled=True)[0]
    squares = summed[:, heads_here : heads_here + 1]
    joined = (summed[:, :heads_here] * lax.rsqrt(squares / width + norm_eps)).astype(jnp.bfloat16)
    joined = lax.all_to_all(joined, "gy", split_axis=0, concat_axis=0, tiled=True)
    joined = joined.reshape(inner * heads_here, tile, HD)

    heads = attend(joined, cosine, sine, cache_keys, cache_values, lengths)
    heads = heads.reshape(inner, heads.shape[0] // inner, tile, HD)
    heads = lax.all_to_all(heads, "gy", split_axis=0, concat_axis=0, tiled=True)
    heads = lax.all_gather(heads, "gx", axis=0, tiled=False)
    partial_out = out_partial(heads, w_out)
    done = lax.psum_scatter(partial_out, "gy", scatter_dimension=0, tiled=True)
    done = done.astype(jnp.bfloat16).reshape(-1, STEPS, rows, partial_out.shape[1])
    return tuple(done[:, s].reshape(-1, partial_out.shape[1]) for s in range(STEPS))


def solution(mesh):
    in_specs = (
        P(None, "gx"),
        P(None, "gx"),
        P("gx"),
        P("gx", "gy"),
        P("gy", "gx"),
        P(("gx", "gy"), None, None),
        P(("gx", "gy"), None, None),
        P(("gx", "gy")),
    )
    out_specs = (P("gy", "gx"), P("gy", "gx"))
    return jax.shard_map(body, mesh=mesh, in_specs=in_specs, out_specs=out_specs, check_vma=False)
```
